32 devices in a mesh: groups: 2 (over x), ctx: 16 (over z, y, core).
Axes of the slice: x: 2, y: 2, z: 4, core: 2. Of those that a mesh axis runs over, the one named last changes fastest.
Arguments:
- query_input: bfloat16 [32, 1536], P('groups'), parts along dimension 0, may hold values from -20 to 20
- query_gain: bfloat16 [1536], replicated, may hold values from 0.5 to 1.5
- nope_weight: bfloat16 [1536, 4096], P(None, 'ctx'), may hold values from -0.15625 to 0.15625
- rope_weight: bfloat16 [1536, 2048], P(None, 'ctx'), may hold values from -0.15625 to 0.15625
- key_up: bfloat16 [32, 128, 512], P('ctx'), may hold values from -0.5 to 0.5
- value_up: bfloat16 [32, 512, 128], P('ctx'), may hold values from -1 to 1
- out_weight: bfloat16 [4096, 7168], P('ctx'), may hold values from -0.09375 to 0.09375
- cache_latent: bfloat16 [4, 32768, 512], P('groups', 'ctx'), parts along dimension 0, may hold values from -8 to 8
- cache_rope: bfloat16 [4, 64, 32768], P('groups', None, 'ctx'), parts along dimension 0, may hold values from -256 to 256
- cached_length: int32 [4], P('groups'), parts along dimension 0, may hold values from 16384 to 32760, as said below
Outputs:
- attn_out: bfloat16 [32, 7168], P('groups'), parts along dimension 0
The draws below stay inside these ranges and needn't reach their ends.
There are 2 independent parts, one for each index of `groups`. The reference program is written for one: setup_inputs(seed, part) draws one part's arguments, and reference() takes and returns one part's arrays. A program takes and returns all parts, laid end to end along the dimension named above; an argument that names none is the same for every part. Nothing has to cross between parts.
Inputs may be any that keep to these rules, and one draw needn't show every extreme that they name: `cached_length`: in every part one request has exactly 32760, so that its last new token sees the cache's last position.
All inputs are finite; a program needn't handle non-finite values.
Results may differ from the reference program's by a relative error of at most 0.012.
Values may be sent and summed in bfloat16 or wider, within the bound.
A program may use at most 128 MiB of HBM per device.

```python
import math
import jax
import jax.numpy as jnp
from jax import lax

D = 7168
QR = 1536
NOPE = 128
ROPE = 64
LAT = 512
VDIM = 128
REQS = 2
STRETCH = 8
CTX_DEV = 2048
HEADS = 32
ROWS = 16
CACHE = 32768
N_CTX = 16


def key_scales(key, smallest, widest):
    spread = jax.random.uniform(jax.random.fold_in(key, 11), (REQS, CACHE), jnp.float32)
    return jnp.exp(jnp.log(smallest) + spread * jnp.log(widest))


def latent_region(key):
    mode_count = 2 * (CACHE // CTX_DEV)
    phases = jax.random.uniform(jax.random.fold_in(key, 13), (REQS, 1, mode_count), jnp.float32) * (2.0 * math.pi)
    vectors = jax.random.normal(jax.random.fold_in(key, 14), (REQS, mode_count, LAT), jnp.float32)
    frequency = (jnp.arange(mode_count, dtype=jnp.float32) + 1.0) * (math.pi / CACHE)
    position = jnp.arange(CACHE, dtype=jnp.float32)
    wave_table = jnp.cos(position[None, :, None] * frequency[None, None, :] + phases) * math.sqrt(2.0 / mode_count)
    return jnp.einsum('bpk,bkl->bpl', wave_table, vectors)


def draw_query_input(key, part):
    spread = jax.random.uniform(jax.random.fold_in(key, 41), (ROWS, 1), jnp.float32)
    row_scale = jnp.exp(jnp.log(0.3) + spread * jnp.log(10.0))
    entries = jax.random.normal(jax.random.fold_in(key, 42), (ROWS, QR), jnp.float32)
    return jnp.clip(entries * row_scale, -20.0, 20.0).astype(jnp.bfloat16)


def draw_cache_latent(key, part):
    scales = key_scales(key, 0.08, 5.0)
    entries = jax.random.normal(jax.random.fold_in(key, 21), (REQS, CACHE, LAT), jnp.float32)
    scaled = (entries + latent_region(key)) * scales[:, :, None]
    return jnp.clip(scaled, -8.0, 8.0).astype(jnp.bfloat16)


def draw_cache_rope(key, part):
    chosen = jax.random.randint(jax.random.fold_in(key, 32), (REQS, 8), 0, CACHE // 2)
    marked = jnp.any(jnp.arange(CACHE, dtype=jnp.int32)[None, None, :] == chosen[:, :, None], axis=1)
    sink_strength = 0.65 * math.log(CACHE)
    scales = key_scales(key, 0.08, 5.0)
    entries = jax.random.normal(jax.random.fold_in(key, 31), (REQS, ROPE, CACHE), jnp.float32)
    scaled = jnp.where(marked[:, None, :], entries * sink_strength, entries * scales[:, None, :])
    return jnp.clip(scaled, -256.0, 256.0).astype(jnp.bfloat16)


def draw_cached_length(key, part):
    longest = jax.random.randint(jax.random.fold_in(key, 51), (), 0, REQS)
    others = jax.random.randint(jax.random.fold_in(key, 52), (REQS,), CACHE // 2, CACHE - STRETCH + 1)
    return jnp.where(jnp.arange(REQS, dtype=jnp.int32) == longest, CACHE - STRETCH, others).astype(jnp.int32)


def block_scale(stream_key, extent, cuts, low, high):
    loudness, own = 1.0, jax.random.fold_in(stream_key, 6)
    for axis_at, blocks in cuts:
        heights = jnp.exp(jax.random.uniform(jax.random.fold_in(own, axis_at), (blocks,), jnp.float32, low / len(cuts), high / len(cuts)))
        loudness = loudness * jnp.repeat(heights, extent[axis_at] // blocks).reshape([-1 if axis == axis_at else 1 for axis in range(len(extent))])
    return loudness


def noise(key, extent, width, most, split=(), held_as=jnp.bfloat16):
    factor_of = block_scale(key, extent, split, -0.22, 0.18) if split else 1.0
    result = jax.random.normal(key, extent, jnp.float32) * width * factor_of
    return jnp.minimum(jnp.maximum(result, -most), most).astype(held_as)


def setup_inputs(seed: int = 0, part: int = 0) -> dict:
    splits = jax.random.split(jax.random.key(seed), 11)
    part_keys = jax.random.split(jax.random.fold_in(splits[10], part), 11)
    return {
        "query_input": draw_query_input(jax.random.fold_in(jax.random.fold_in(splits[10], part), 71), part),
        "query_gain": jnp.clip(1.0 + 0.1 * jax.random.normal(splits[1], (QR,), jnp.float32), 0.5, 1.5).astype(jnp.bfloat16),
        "nope_weight": noise(splits[2], (QR, HEADS * NOPE), QR ** -0.5, 0.15625, ((1, 16),)),
        "rope_weight": noise(splits[3], (QR, HEADS * ROPE), QR ** -0.5, 0.15625, ((1, 16),)),
        "key_up": noise(splits[4], (HEADS, NOPE, LAT), NOPE ** -0.5, 0.5, ((0, 16),)),
        "value_up": noise(splits[5], (HEADS, LAT, VDIM), (LAT // 16) ** -0.5, 1.0, ((0, 16),)),
        "out_weight": noise(splits[6], (HEADS * VDIM, D), (HEADS * VDIM) ** -0.5, 0.09375, ((0, 16),)),
        "cache_latent": draw_cache_latent(jax.random.fold_in(jax.random.fold_in(splits[10], part), 71), part),
        "cache_rope": draw_cache_rope(jax.random.fold_in(jax.random.fold_in(splits[10], part), 71), part),
        "cached_length": draw_cached_length(jax.random.fold_in(jax.random.fold_in(splits[10], part), 71), part),
    }


mscale_yarn = 1.0 + 0.1 * math.log(40.0)
masked_score = -1e+30

def reference(query_input, query_gain, nope_weight, rope_weight, key_up, value_up, out_weight, cache_latent, cache_rope, cached_length):
    widened = query_input.astype(jnp.float32)
    normed = (widened * lax.rsqrt(lax.optimization_barrier(jnp.mean(widened * widened, axis=-1, keepdims=True)) + 1e-06) * query_gain.astype(jnp.float32)).astype(jnp.bfloat16)
    query_nope = jnp.dot(normed, nope_weight, preferred_element_type=jnp.float32).astype(jnp.bfloat16).reshape(ROWS, HEADS, NOPE)
    query_rope = jnp.dot(normed, rope_weight, preferred_element_type=jnp.float32).astype(jnp.bfloat16).reshape(ROWS, HEADS, ROPE)
    query_latent = jnp.einsum('rhn,hnl->rhl', query_nope.astype(jnp.float32), key_up.astype(jnp.float32)).astype(jnp.bfloat16)
    softmax_scale = mscale_yarn * mscale_yarn / math.sqrt(NOPE + ROPE)
    latent_rows = query_latent.astype(jnp.float32).reshape(REQS, STRETCH, HEADS, LAT)
    rope_rows = query_rope.astype(jnp.float32).reshape(REQS, STRETCH, HEADS, ROPE)
    last_seen = cached_length.astype(jnp.int32)[:, None] + jnp.arange(STRETCH, dtype=jnp.int32)[None, :]

    def one_block(running, block):
        row_top, weight_sum, pooled = running
        first_key = (block * CTX_DEV).astype(jnp.int32)
        key_block = lax.dynamic_slice_in_dim(cache_latent, first_key, CTX_DEV, 1).astype(jnp.float32)
        rope_block = lax.dynamic_slice_in_dim(cache_rope, first_key, CTX_DEV, 2).astype(jnp.float32)
        positions = first_key + jnp.arange(CTX_DEV, dtype=jnp.int32)
        scores = softmax_scale * (jnp.einsum('bchl,bpl->bchp', latent_rows, key_block) + jnp.einsum('bche,bep->bchp', rope_rows, rope_block))
        visible = (positions[None, None, :] <= last_seen[:, :, None])[:, :, None, :]
        scores = jnp.where(visible, scores, masked_score)
        block_peak = lax.optimization_barrier(jnp.max(scores, axis=-1))
        weights = jnp.where(visible, jnp.exp(scores - block_peak[..., None]), 0.0)
        rounded = lax.optimization_barrier(weights.astype(jnp.bfloat16)).astype(jnp.float32)
        block_sum = lax.optimization_barrier(jnp.sum(weights, axis=-1))
        block_pool = jnp.einsum('bchp,bpl->bchl', rounded, key_block)
        new_top = jnp.maximum(row_top, block_peak)
        keep_old = jnp.exp(row_top - new_top)
        keep_new = jnp.exp(block_peak - new_top)
        weight_sum = weight_sum * keep_old + block_sum * keep_new
        pooled = pooled * keep_old[..., None] + block_pool * keep_new[..., None]
        return ((new_top, weight_sum, pooled), None)
    initial = (jnp.full((REQS, STRETCH, HEADS), masked_score, jnp.float32), jnp.zeros((REQS, STRETCH, HEADS), jnp.float32), jnp.zeros((REQS, STRETCH, HEADS, LAT), jnp.float32))
    finals, unused = lax.scan(one_block, initial, jnp.arange(N_CTX, dtype=jnp.int32))
    row_top, weight_sum, pooled = finals
    attended = (pooled / weight_sum[..., None]).astype(jnp.bfloat16).reshape(ROWS, HEADS, LAT)
    head_values = jnp.einsum('rhl,hlv->rhv', attended.astype(jnp.float32), value_up.astype(jnp.float32)).astype(jnp.bfloat16).reshape(ROWS, HEADS * VDIM)
    return jnp.dot(head_values, out_weight, preferred_element_type=jnp.float32).astype(jnp.bfloat16)
```

```python
import functools
import math

import jax
import jax.numpy as jnp
from jax import lax
from jax.experimental import pallas as pl
from jax.experimental.pallas import tpu as pltpu
from jax.sharding import PartitionSpec as P

mscale_yarn = 1.0 + 0.1 * math.log(40.0)
masked_score = -1e30
MESH = pl.DeviceIdType.MESH
F32 = jnp.float32
BF16 = jnp.bfloat16
NT = (((1,), (1,)), ((), ()))


def kernel(
    n, tile,
    x_hbm, gain_ref, nope_hbm, ropew_hbm, kup_hbm, vup_hbm, outw_hbm, lat_hbm, crope_hbm, len_ref,
    out_ref,
    x_v, nope_v, ropew_v, kup_v, vup_v, outw_v, lat_v, crope_v,
    qbuf, score_s, peak_s, sum_s, pool_s, pk_buf, sm_buf,
    sb1, rb1, sb2, rb2, sb3, rb3,
    opart, ob1, or1, os2, or2, os3, or3, fin,
    ld_sem,
    q1s, q1r, q2s, q2r, q3s, q3r,
    pks, pkr, sms, smr,
    p1s, p1r, p2s, p2r, p3s, p3r,
    o1s, o1r, o2s, o2r, o3s, o3r,
    f1s, f1r, f2s, f2r, f3s, f3r,
):
    me = lax.axis_index("ctx")
    outer = n // 4
    a, y, c = me // 4, (me // 2) % 2, me % 2
    heads, nope_w, lat_w = kup_v.shape
    rows = x_v.shape[0]
    requests, keys, _ = lat_v.shape
    stretch = rows // requests
    block_rows = heads * stretch
    rope_all = ropew_v.shape[1]
    rope_w = rope_all // heads
    scale = mscale_yarn * mscale_yarn / math.sqrt(nope_w + rope_w)

    def dev(ai, yi, ci):
        return ai * 4 + yi * 2 + ci

    def far(k):
        return (a + k) % outer

    def back(k):
        return (a + outer - k) % outer

    def remote(src, dst, ssem, rsem, target):
        return pltpu.make_async_remote_copy(
            src_ref=src, dst_ref=dst, send_sem=ssem, recv_sem=rsem,
            device_id={"ctx": target}, device_id_type=MESH,
        )

    loads = []

    def load(src, dst):
        copy = pltpu.make_async_copy(src, dst, ld_sem.at[len(loads)])
        copy.start()
        loads.append(copy)
        return copy

    load_x = load(x_hbm, x_v)
    load_nope = load(nope_hbm, nope_v)
    load_rope = load(ropew_hbm, ropew_v)
    load_kup = load(kup_hbm, kup_v)
    load_cache = [load(lat_hbm, lat_v)]
    for h in range(heads):
        load_cache.append(load(crope_hbm, crope_v.at[:, h * rope_w : (h + 1) * rope_w, :]))
    load_vup = load(vup_hbm, vup_v)
    load_outw = load(outw_hbm, outw_v)

    barrier = pltpu.get_barrier_semaphore()
    for k in range(1, n):
        pl.semaphore_signal(
            barrier, inc=1, device_id={"ctx": (me + k) % n}, device_id_type=MESH
        )

    load_x.wait()
    widened = x_v[...].astype(F32)
    normed = (
        widened
        * lax.rsqrt(jnp.mean(widened * widened, axis=-1, keepdims=True) + 1e-06)
        * gain_ref[...]
    ).astype(BF16)
    load_nope.wait()
    query_nope = jnp.dot(normed, nope_v[...], preferred_element_type=F32).astype(BF16)
    load_rope.wait()
    query_rope = jnp.dot(normed, ropew_v[...], preferred_element_type=F32)
    load_kup.wait()
    latents = [
        jnp.dot(
            query_nope[:, h * nope_w : (h + 1) * nope_w], kup_v[h], preferred_element_type=F32
        )
        for h in range(heads)
    ]
    lane_head = lax.broadcasted_iota(jnp.int32, (stretch, rope_all), 1) // rope_w
    for b in range(requests):
        part = slice(b * stretch, (b + 1) * stretch)
        qbuf[me, b, :, :lat_w] = jnp.concatenate([t[part] for t in latents], axis=0).astype(BF16)
        qbuf[me, b, :, lat_w:] = jnp.concatenate(
            [jnp.where(lane_head == h, query_rope[part], 0.0) for h in range(heads)], axis=0
        ).astype(BF16)
    pl.semaphore_wait(barrier, n - 1)

    pending = []

    def send(copy):
        copy.start()
        pending.append(copy)

    def gather(at, s1, r1, s2, r2, s3, r3):
        def to_far(k):
            ref = at(a, y, c)
            return remote(ref, ref, s1.at[k], r1.at[k], dev(far(k), y, c))

        def from_far(k):
            ref = at(back(k), y, c)
            return remote(ref, ref, s1.at[k], r1.at[k], dev(far(k), y, c))

        def to_y(k, yy):
            ref = at(back(k), yy, c)
            return remote(ref, ref, s2.at[k], r2.at[k], dev(a, 1 - y, c))

        def to_core(k, j, cc):
            ref = at(back(k), (y + j) % 2, cc)
            return remote(ref, ref, s3.at[2 * k + j], r3.at[2 * k + j], dev(a, y, 1 - c))

        for k in range(1, outer):
            send(to_far(k))
        send(to_y(0, y))
        send(to_core(0, 0, c))
        for k in range(1, outer):
            from_far(k).wait_recv()
            send(to_y(k, y))
            send(to_core(k, 0, c))
            to_y(k - 1, 1 - y).wait_recv()
            send(to_core(k - 1, 1, c))
        to_y(outer - 1, 1 - y).wait_recv()
        send(to_core(outer - 1, 1, c))
        for k in range(outer):
            for j in range(2):
                to_core(k, j, 1 - c).wait_recv()

    gather(lambda ai, yi, ci: qbuf.at[dev(ai, yi, ci)], q1s, q1r, q2s, q2r, q3s, q3r)

    for copy in load_cache:
        copy.wait()
    first_key = me * keys
    tile_devs = tile // block_rows
    tiles_per = n // tile_devs
    tiles = requests * tiles_per

    def each_tile(body):
        if tiles <= 2:
            for t in range(tiles):
                body(t, t // tiles_per, (t % tiles_per) * tile_devs, t * tile)
        else:
            def step(t, carry):
                body(
                    t, t // tiles_per, (t % tiles_per) * tile_devs,
                    pl.multiple_of(t * tile, tile),
                )
                return carry
            lax.fori_loop(0, tiles, step, 0)

    def compact(column):
        return jnp.transpose(jnp.broadcast_to(column, (tile, 128)))[0:1, :]

    def spread(row):
        return jnp.transpose(jnp.broadcast_to(row, (128, tile)))[:, 0:1]

    def scores_of(t, b, d0, r0):
        query = qbuf[pl.ds(d0, tile_devs), b].reshape(tile, lat_w + rope_all)
        raw = lax.dot_general(query[:, :lat_w], lat_v[b], NT, preferred_element_type=F32)
        raw = raw + jnp.dot(query[:, lat_w:], crope_v[b], preferred_element_type=F32)
        row = lax.broadcasted_iota(jnp.int32, (tile, 1), 0) % stretch
        limit = len_ref[b] + row - first_key
        where_key = lax.broadcasted_iota(jnp.int32, (tile, keys), 1)
        raw = jnp.where(where_key <= limit, raw, masked_score)
        score_s[t] = raw
        peak = jnp.max(raw, axis=1, keepdims=True)
        peak_s[pl.ds(r0, tile), :] = jnp.broadcast_to(peak, (tile, 128))
        pk_buf[me, :, pl.ds(r0, tile)] = compact(peak)

    each_tile(scores_of)

    def share(buf, ss, rs):
        for k in range(1, n):
            send(remote(buf.at[me], buf.at[me], ss.at[k], rs.at[k], (me + k) % n))

    def shared(buf, ss, rs):
        for k in range(1, n):
            ref = buf.at[(me + n - k) % n]
            remote(ref, ref, ss.at[k], rs.at[k], (me + k) % n).wait_recv()

    share(pk_buf, pks, pkr)

    def pool_of(t, b, d0, r0):
        peak = peak_s[pl.ds(r0, tile), 0:1]
        weights = jnp.exp((score_s[t] - peak) * scale)
        sum_s[pl.ds(r0, tile), :] = jnp.broadcast_to(
            jnp.sum(weights, axis=1, keepdims=True), (tile, 128)
        )
        pool_s[b, pl.ds(d0, tile_devs)] = jnp.dot(
            weights.astype(BF16), lat_v[b], preferred_element_type=F32
        ).reshape(tile_devs, block_rows, lat_w)

    each_tile(pool_of)
    shared(pk_buf, pks, pkr)

    def rescale(t, b, d0, r0):
        top = jnp.max(pk_buf[:, :, pl.ds(r0, tile)], axis=0)
        factor = jnp.exp((peak_s[pl.ds(r0, tile), 0:1] - spread(top)) * scale)
        sm_buf[me, :, pl.ds(r0, tile)] = compact(sum_s[pl.ds(r0, tile), 0:1] * factor)
        scaled = pool_s[b, pl.ds(d0, tile_devs)].reshape(tile, lat_w) * factor
        scaled = scaled.reshape(tile_devs, block_rows, lat_w)
        pool_s[b, pl.ds(d0, tile_devs)] = scaled
        sb1[pl.ds(d0, tile_devs), b] = scaled.astype(BF16)

    each_tile(rescale)

    def to_core(ka, j):
        slot = 2 * ka + j
        return remote(
            sb1.at[dev(far(ka), (y + j) % 2, 1 - c)], rb1.at[slot],
            p1s.at[slot], p1r.at[slot], dev(a, y, 1 - c),
        )

    def to_y(ka):
        return remote(sb2.at[ka], rb2.at[ka], p2s.at[ka], p2r.at[ka], dev(a, 1 - y, c))

    def to_far(ka):
        return remote(sb3.at[ka], rb3.at[ka], p3s.at[ka], p3r.at[ka], dev(far(ka), y, c))

    order = list(range(1, outer)) + [0]
    for j in (1, 0):
        for ka in order:
            send(to_core(ka, j))
    share(sm_buf, sms, smr)
    for ka in order:
        to_core(ka, 1).wait_recv()
        d = dev(far(ka), 1 - y, c)
        sb2[ka] = (pool_s[:, d] + rb1[2 * ka + 1].astype(F32)).astype(BF16)
        send(to_y(ka))
    for ka in order:
        to_core(ka, 0).wait_recv()
        to_y(ka).wait_recv()
        total = pool_s[:, dev(far(ka), y, c)] + rb1[2 * ka].astype(F32) + rb2[ka].astype(F32)
        if ka:
            sb3[ka] = total.astype(BF16)
            send(to_far(ka))
    for ka in range(1, outer):
        to_far(ka).wait_recv()
        total = total + rb3[ka].astype(F32)
    shared(sm_buf, sms, smr)

    all_sums = jnp.sum(sm_buf[...], axis=0)
    per_request = n * block_rows
    owner = lax.broadcasted_iota(jnp.int32, (block_rows, per_request), 1)
    mine = owner == me * block_rows + lax.broadcasted_iota(
        jnp.int32, (block_rows, per_request), 0
    )
    attended = []
    for b in range(requests):
        sums = jnp.sum(
            jnp.where(mine, all_sums[:, b * per_request : (b + 1) * per_request], 0.0),
            axis=1, keepdims=True,
        )
        attended.append(total[b] / sums)
    load_vup.wait()
    values = []
    for h in range(heads):
        stacked = jnp.concatenate(
            [t[h * stretch : (h + 1) * stretch] for t in attended], axis=0
        ).astype(BF16)
        values.append(jnp.dot(stacked, vup_v[h], preferred_element_type=F32).astype(BF16))
    head_values = jnp.concatenate(values, axis=1)

    half = rows // 2
    width = opart.shape[3]
    model = out_ref.shape[1]

    def to_core_out(q):
        return remote(ob1.at[q, 1 - c], or1.at[q], o1s.at[q], o1r.at[q], dev(a, y, 1 - c))

    def to_y_out(ka):
        return remote(os2.at[ka], or2.at[ka], o2s.at[ka], o2r.at[ka], dev(a, 1 - y, c))

    def to_far_out(ka):
        return remote(os3.at[ka], or3.at[ka], o3s.at[ka], o3r.at[ka], dev(far(ka), y, c))

    load_outw.wait()
    for q in range(n // 2):
        used = max(0, min(width, model - q * width))
        if used < width:
            opart[q] = jnp.zeros((2, half, width), F32)
            ob1[q] = jnp.zeros((2, half, width), BF16)
        if used:
            partial = jnp.dot(
                head_values, outw_v[:, q * width : q * width + used], preferred_element_type=F32
            )
            for side in range(2):
                piece = partial[side * half : (side + 1) * half]
                opart[q, side, :, :used] = piece
                ob1[q, side, :, :used] = piece.astype(BF16)
        send(to_core_out(q))
    for ka in order:
        q = far(ka) * 2 + (1 - y)
        to_core_out(q).wait_recv()
        os2[ka] = (opart[q, c] + or1[q].astype(F32)).astype(BF16)
        send(to_y_out(ka))
    for ka in order:
        q = far(ka) * 2 + y
        to_core_out(q).wait_recv()
        to_y_out(ka).wait_recv()
        summed = opart[q, c] + or1[q].astype(F32) + or2[ka].astype(F32)
        if ka:
            os3[ka] = summed.astype(BF16)
            send(to_far_out(ka))
    for ka in range(1, outer):
        to_far_out(ka).wait_recv()
        summed = summed + or3[ka].astype(F32)
    fin[a * 2 + y, c] = summed.astype(BF16)
    gather(lambda ai, yi, ci: fin.at[ai * 2 + yi, ci], f1s, f1r, f2s, f2r, f3s, f3r)

    for q in range(n // 2):
        used = max(0, min(width, model - q * width))
        if used:
            out_ref[:, q * width : q * width + used] = jnp.concatenate(
                [fin[q, 0, :, :used].astype(F32), fin[q, 1, :, :used].astype(F32)], axis=0
            ).astype(BF16)
    for copy in pending:
        copy.wait_send()


def local(
    n, query_input, query_gain, nope_weight, rope_weight, key_up, value_up, out_weight,
    cache_latent, cache_rope, cached_length,
):
    heads, nope_w, lat_w = key_up.shape
    rows = query_input.shape[0]
    requests, keys, _ = cache_latent.shape
    stretch = rows // requests
    block_rows = heads * stretch
    rope_all = rope_weight.shape[1]
    rope_w = rope_all // heads
    model = out_weight.shape[1]
    outer = n // 4
    flat = requests * n * block_rows
    tile = min(256, n * block_rows)
    half = rows // 2
    lane_tiles = -(-model // 128)
    width = -(-lane_tiles // (n // 2)) * 128
    block = (requests, block_rows, lat_w)
    vmem = pltpu.VMEM
    dma = lambda count: pltpu.SemaphoreType.DMA((count,))
    any_spec = pl.BlockSpec(memory_space=pl.ANY)
    vmem_spec = pl.BlockSpec(memory_space=pltpu.VMEM)
    gather_sems = [dma(outer)] * 4 + [dma(2 * outer)] * 2
    return pl.pallas_call(
        functools.partial(kernel, n, tile),
        out_shape=jax.ShapeDtypeStruct((rows, model), BF16),
        in_specs=[any_spec, vmem_spec] + [any_spec] * 7
        + [pl.BlockSpec(memory_space=pltpu.SMEM)],
        out_specs=vmem_spec,
        scratch_shapes=[
            vmem(query_input.shape, BF16), vmem(nope_weight.shape, BF16),
            vmem(rope_weight.shape, BF16), vmem(key_up.shape, BF16),
            vmem(value_up.shape, BF16), vmem(out_weight.shape, BF16),
            vmem(cache_latent.shape, BF16), vmem((requests, rope_all, keys), BF16),
            vmem((n, requests, block_rows, lat_w + rope_all), BF16),
            vmem((flat // tile, tile, keys), F32),
            vmem((flat, 128), F32), vmem((flat, 128), F32),
            vmem((requests, n, block_rows, lat_w), F32),
            vmem((n, 1, flat), F32), vmem((n, 1, flat), F32),
            vmem((n, *block), BF16), vmem((n // 2, *block), BF16),
            vmem((outer, *block), BF16), vmem((outer, *block), BF16),
            vmem((outer, *block), BF16), vmem((outer, *block), BF16),
            vmem((n // 2, 2, half, width), F32), vmem((n // 2, 2, half, width), BF16),
            vmem((n // 2, half, width), BF16),
            vmem((outer, half, width), BF16), vmem((outer, half, width), BF16),
            vmem((outer, half, width), BF16), vmem((outer, half, width), BF16),
            vmem((n // 2, 2, half, width), BF16),
            dma(7 + heads),
            *gather_sems,
            dma(n), dma(n), dma(n), dma(n),
            dma(n // 2), dma(n // 2), dma(outer), dma(outer), dma(outer), dma(outer),
            dma(n // 2), dma(n // 2), dma(outer), dma(outer), dma(outer), dma(outer),
            *gather_sems,
        ],
        compiler_params=pltpu.CompilerParams(
            collective_id=0, has_side_effects=True, vmem_limit_bytes=63 * 1024 * 1024
        ),
    )(
        query_input, query_gain.astype(F32).reshape(1, -1), nope_weight, rope_weight, key_up,
        value_up, out_weight, cache_latent, cache_rope, cached_length,
    )


def solution(mesh):
    placed = (
        P("groups", None),
        P(),
        P(None, "ctx"),
        P(None, "ctx"),
        P("ctx", None, None),
        P("ctx", None, None),
        P("ctx", None),
        P("groups", "ctx", None),
        P("groups", None, "ctx"),
        P("groups"),
    )
    return jax.shard_map(
        functools.partial(local, mesh.shape["ctx"]), mesh=mesh, in_specs=placed,
        out_specs=P("groups", None), check_vma=False,
    )
```

```python
import functools
import math

import jax
import jax.numpy as jnp
from jax import lax
from jax.experimental import pallas as pl
from jax.experimental.pallas import tpu as pltpu
from jax.sharding import PartitionSpec as P

mscale_yarn = 1.0 + 0.1 * math.log(40.0)
masked_score = -1e30
MESH = pl.DeviceIdType.MESH
F32 = jnp.float32
BF16 = jnp.bfloat16
NT = (((1,), (1,)), ((), ()))


def kernel(
    n, tile,
    x_hbm, gain_ref, nope_hbm, ropew_hbm, kup_hbm, vup_hbm, outw_hbm, lat_hbm, crope_hbm, len_ref,
    out_ref,
    x_v, nope_v, ropew_v, kup_v, vup_v, outw_v, lat_v, crope_v,
    qbuf, score_s, peak_s, sum_s, pool_s, pk_buf, sm_buf,
    sb1, rb1, sb2, rb2,
    opart, ob1, or1, os2, or2, fin,
    ld_sem,
    q1s, q1r, q2s, q2r,
    pks, pkr, sms, smr,
    p1s, p1r, p2s, p2r,
    o1s, o1r, o2s, o2r,
    f1s, f1r, f2s, f2r,
):
    me = lax.axis_index("ctx")
    chips = n // 2
    chip, c = me // 2, me % 2
    heads, nope_w, lat_w = kup_v.shape
    rows = x_v.shape[0]
    requests, keys, _ = lat_v.shape
    stretch = rows // requests
    block_rows = heads * stretch
    rope_all = ropew_v.shape[1]
    rope_w = rope_all // heads
    scale = mscale_yarn * mscale_yarn / math.sqrt(nope_w + rope_w)

    def peer(k):
        flipped, bit = 0, 1
        while bit < chips:
            flipped = flipped + ((chip // bit + (k // bit) % 2) % 2) * bit
            bit *= 2
        return flipped

    def remote(src, dst, ssem, rsem, target):
        return pltpu.make_async_remote_copy(
            src_ref=src, dst_ref=dst, send_sem=ssem, recv_sem=rsem,
            device_id={"ctx": target}, device_id_type=MESH,
        )

    loads = []

    def load(src, dst):
        copy = pltpu.make_async_copy(src, dst, ld_sem.at[len(loads)])
        copy.start()
        loads.append(copy)
        return copy

    load_x = load(x_hbm, x_v)
    load_nope = load(nope_hbm, nope_v)
    load_rope = load(ropew_hbm, ropew_v)
    load_kup = load(kup_hbm, kup_v)
    barrier = pltpu.get_barrier_semaphore()
    for k in range(1, n):
        pl.semaphore_signal(
            barrier, inc=1, device_id={"ctx": (me + k) % n}, device_id_type=MESH
        )

    load_x.wait()
    widened = x_v[...].astype(F32)
    normed = (
        widened
        * lax.rsqrt(jnp.mean(widened * widened, axis=-1, keepdims=True) + 1e-06)
        * gain_ref[...].astype(F32).reshape(1, -1)
    ).astype(BF16)
    load_nope.wait()
    query_nope = jnp.dot(normed, nope_v[...], preferred_element_type=F32).astype(BF16)
    load_rope.wait()
    query_rope = jnp.dot(normed, ropew_v[...], preferred_element_type=F32)
    load_kup.wait()
    load_cache = [load(lat_hbm, lat_v)]
    for h in range(heads):
        load_cache.append(load(crope_hbm, crope_v.at[:, h * rope_w : (h + 1) * rope_w, :]))
    load_vup = load(vup_hbm, vup_v)
    load_outw = load(outw_hbm, outw_v)
    latents = [
        jnp.dot(
            query_nope[:, h * nope_w : (h + 1) * nope_w], kup_v[h], preferred_element_type=F32
        )
        for h in range(heads)
    ]
    lane_head = lax.broadcasted_iota(jnp.int32, (stretch, rope_all), 1) // rope_w
    for b in range(requests):
        part = slice(b * stretch, (b + 1) * stretch)
        qbuf[me, b, :, :lat_w] = jnp.concatenate([t[part] for t in latents], axis=0).astype(BF16)
        qbuf[me, b, :, lat_w:] = jnp.concatenate(
            [jnp.where(lane_head == h, query_rope[part], 0.0) for h in range(heads)], axis=0
        ).astype(BF16)
    pl.semaphore_wait(barrier, n - 1)

    pending = []

    def send(copy):
        copy.start()
        pending.append(copy)

    def gather(at, s1, r1, s2, r2):
        def to_chip(k, source):
            ref = at(source, c)
            return remote(ref, ref, s1.at[k], r1.at[k], peer(k) * 2 + c)

        def to_core(k, side):
            ref = at(peer(k), side)
            return remote(ref, ref, s2.at[k], r2.at[k], chip * 2 + 1 - c)

        for k in range(1, chips):
            send(to_chip(k, chip))
        send(to_core(0, c))
        for k in range(1, chips):
            to_chip(k, peer(k)).wait_recv()
            send(to_core(k, c))
        for k in range(chips):
            to_core(k, 1 - c).wait_recv()

    gather(lambda at_chip, side: qbuf.at[at_chip * 2 + side], q1s, q1r, q2s, q2r)

    for copy in load_cache:
        copy.wait()
    first_key = me * keys
    tile_devs = tile // block_rows
    tiles_per = n // tile_devs
    tiles = requests * tiles_per

    def each_tile(body):
        if tiles <= 2:
            for t in range(tiles):
                body(t, t // tiles_per, (t % tiles_per) * tile_devs, t * tile)
        else:
            def step(t, carry):
                body(
                    t, t // tiles_per, (t % tiles_per) * tile_devs,
                    pl.multiple_of(t * tile, tile),
                )
                return carry
            lax.fori_loop(0, tiles, step, 0)

    def compact(column):
        return jnp.transpose(jnp.broadcast_to(column, (tile, 128)))[0:1, :]

    def spread(row):
        return jnp.transpose(jnp.broadcast_to(row, (128, tile)))[:, 0:1]

    def scores_of(t, b, d0, r0):
        query = qbuf[pl.ds(d0, tile_devs), b].reshape(tile, lat_w + rope_all)
        raw = lax.dot_general(query[:, :lat_w], lat_v[b], NT, preferred_element_type=F32)
        raw = raw + jnp.dot(query[:, lat_w:], crope_v[b], preferred_element_type=F32)
        row = lax.broadcasted_iota(jnp.int32, (tile, 1), 0) % stretch
        limit = len_ref[b] + row - first_key
        where_key = lax.broadcasted_iota(jnp.int32, (tile, keys), 1)
        raw = jnp.where(where_key <= limit, raw, masked_score)
        score_s[t] = raw
        peak = jnp.max(raw, axis=1, keepdims=True)
        peak_s[pl.ds(r0, tile), :] = jnp.broadcast_to(peak, (tile, 128))
        pk_buf[me, :, pl.ds(r0, tile)] = compact(peak)

    each_tile(scores_of)

    def share(buf, ss, rs):
        for k in range(1, n):
            send(remote(buf.at[me], buf.at[me], ss.at[k], rs.at[k], (me + k) % n))

    def shared(buf, ss, rs):
        for k in range(1, n):
            ref = buf.at[(me + n - k) % n]
            remote(ref, ref, ss.at[k], rs.at[k], (me + k) % n).wait_recv()

    share(pk_buf, pks, pkr)

    def pool_of(t, b, d0, r0):
        peak = peak_s[pl.ds(r0, tile), 0:1]
        weights = jnp.exp((score_s[t] - peak) * scale)
        sum_s[pl.ds(r0, tile), :] = jnp.broadcast_to(
            jnp.sum(weights, axis=1, keepdims=True), (tile, 128)
        )
        pool_s[b, pl.ds(d0, tile_devs)] = jnp.dot(
            weights.astype(BF16), lat_v[b], preferred_element_type=F32
        ).reshape(tile_devs, block_rows, lat_w)

    each_tile(pool_of)
    shared(pk_buf, pks, pkr)

    def rescale(t, b, d0, r0):
        top = jnp.max(pk_buf[:, :, pl.ds(r0, tile)], axis=0)
        factor = jnp.exp((peak_s[pl.ds(r0, tile), 0:1] - spread(top)) * scale)
        sm_buf[me, :, pl.ds(r0, tile)] = compact(sum_s[pl.ds(r0, tile), 0:1] * factor)
        scaled = pool_s[b, pl.ds(d0, tile_devs)].reshape(tile, lat_w) * factor
        scaled = scaled.reshape(tile_devs, block_rows, lat_w)
        pool_s[b, pl.ds(d0, tile_devs)] = scaled
        sb1[pl.ds(d0, tile_devs), b] = scaled.astype(BF16)

    each_tile(rescale)

    def to_core(k):
        return remote(
            sb1.at[peer(k) * 2 + 1 - c], rb1.at[k], p1s.at[k], p1r.at[k], chip * 2 + 1 - c
        )

    def to_chip(k):
        return remote(sb2.at[k], rb2.at[k], p2s.at[k], p2r.at[k], peer(k) * 2 + c)

    order = list(range(1, chips)) + [0]
    for k in order:
        send(to_core(k))
    share(sm_buf, sms, smr)
    for k in order:
        to_core(k).wait_recv()
        total = pool_s[:, peer(k) * 2 + c] + rb1[k].astype(F32)
        if k:
            sb2[k] = total.astype(BF16)
            send(to_chip(k))
    for k in range(1, chips):
        to_chip(k).wait_recv()
        total = total + rb2[k].astype(F32)
    shared(sm_buf, sms, smr)

    all_sums = jnp.sum(sm_buf[...], axis=0)
    per_request = n * block_rows
    owner = lax.broadcasted_iota(jnp.int32, (block_rows, per_request), 1)
    mine = owner == me * block_rows + lax.broadcasted_iota(
        jnp.int32, (block_rows, per_request), 0
    )
    attended = []
    for b in range(requests):
        sums = jnp.sum(
            jnp.where(mine, all_sums[:, b * per_request : (b + 1) * per_request], 0.0),
            axis=1, keepdims=True,
        )
        attended.append(total[b] / sums)
    load_vup.wait()
    values = []
    for h in range(heads):
        stacked = jnp.concatenate(
            [t[h * stretch : (h + 1) * stretch] for t in attended], axis=0
        ).astype(BF16)
        values.append(jnp.dot(stacked, vup_v[h], preferred_element_type=F32).astype(BF16))
    head_values = jnp.concatenate(values, axis=1)

    half = rows // 2
    width = opart.shape[3]
    model = out_ref.shape[1]

    def to_core_out(q):
        return remote(
            ob1.at[q, 1 - c], or1.at[q], o1s.at[q], o1r.at[q], chip * 2 + 1 - c
        )

    def to_chip_out(k):
        return remote(os2.at[k], or2.at[k], o2s.at[k], o2r.at[k], peer(k) * 2 + c)

    load_outw.wait()
    for q in range(chips):
        used = max(0, min(width, model - q * width))
        if used < width:
            opart[q] = jnp.zeros((2, half, width), F32)
            ob1[q] = jnp.zeros((2, half, width), BF16)
        if used:
            partial = jnp.dot(
                head_values, outw_v[:, q * width : q * width + used], preferred_element_type=F32
            )
            for side in range(2):
                piece = partial[side * half : (side + 1) * half]
                opart[q, side, :, :used] = piece
                ob1[q, side, :, :used] = piece.astype(BF16)
        send(to_core_out(q))
    for k in order:
        q = peer(k)
        to_core_out(q).wait_recv()
        summed = opart[q, c] + or1[q].astype(F32)
        if k:
            os2[k] = summed.astype(BF16)
            send(to_chip_out(k))
    for k in range(1, chips):
        to_chip_out(k).wait_recv()
        summed = summed + or2[k].astype(F32)
    fin[chip, c] = summed.astype(BF16)
    gather(lambda at_chip, side: fin.at[at_chip, side], f1s, f1r, f2s, f2r)

    for q in range(chips):
        used = max(0, min(width, model - q * width))
        if used:
            out_ref[:, q * width : q * width + used] = jnp.concatenate(
                [fin[q, 0, :, :used].astype(F32), fin[q, 1, :, :used].astype(F32)], axis=0
            ).astype(BF16)
    for copy in pending:
        copy.wait_send()


def local(
    n, query_input, query_gain, nope_weight, rope_weight, key_up, value_up, out_weight,
    cache_latent, cache_rope, cached_length,
):
    heads, nope_w, lat_w = key_up.shape
    rows = query_input.shape[0]
    requests, keys, _ = cache_latent.shape
    stretch = rows // requests
    block_rows = heads * stretch
    rope_all = rope_weight.shape[1]
    rope_w = rope_all // heads
    model = out_weight.shape[1]
    chips = n // 2
    flat = requests * n * block_rows
    tile = min(256, n * block_rows)
    half = rows // 2
    lane_tiles = -(-model // 128)
    width = -(-lane_tiles // chips) * 128
    block = (requests, block_rows, lat_w)
    vmem = pltpu.VMEM
    dma = lambda count: pltpu.SemaphoreType.DMA((count,))
    any_spec = pl.BlockSpec(memory_space=pl.ANY)
    vmem_spec = pl.BlockSpec(memory_space=pltpu.VMEM)
    sems = [dma(chips)] * 4
    return pl.pallas_call(
        functools.partial(kernel, n, tile),
        out_shape=jax.ShapeDtypeStruct((rows, model), BF16),
        in_specs=[any_spec, vmem_spec] + [any_spec] * 7
        + [pl.BlockSpec(memory_space=pltpu.SMEM)],
        out_specs=vmem_spec,
        scratch_shapes=[
            vmem(query_input.shape, BF16), vmem(nope_weight.shape, BF16),
            vmem(rope_weight.shape, BF16), vmem(key_up.shape, BF16),
            vmem(value_up.shape, BF16), vmem(out_weight.shape, BF16),
            vmem(cache_latent.shape, BF16), vmem((requests, rope_all, keys), BF16),
            vmem((n, requests, block_rows, lat_w + rope_all), BF16),
            vmem((flat // tile, tile, keys), F32),
            vmem((flat, 128), F32), vmem((flat, 128), F32),
            vmem((requests, n, block_rows, lat_w), F32),
            vmem((n, 1, flat), F32), vmem((n, 1, flat), F32),
            vmem((n, *block), BF16), vmem((chips, *block), BF16),
            vmem((chips, *block), BF16), vmem((chips, *block), BF16),
            vmem((chips, 2, half, width), F32), vmem((chips, 2, half, width), BF16),
            vmem((chips, half, width), BF16), vmem((chips, half, width), BF16),
            vmem((chips, half, width), BF16), vmem((chips, 2, half, width), BF16),
            dma(7 + heads),
            *sems, dma(n), dma(n), dma(n), dma(n), *sems, *sems, *sems,
        ],
        compiler_params=pltpu.CompilerParams(
            collective_id=0, has_side_effects=True, vmem_limit_bytes=63 * 1024 * 1024
        ),
    )(
        query_input, query_gain, nope_weight, rope_weight, key_up,
        value_up, out_weight, cache_latent, cache_rope, cached_length,
    )


def solution(mesh):
    placed = (
        P("groups", None),
        P(),
        P(None, "ctx"),
        P(None, "ctx"),
        P("ctx", None, None),
        P("ctx", None, None),
        P("ctx", None),
        P("groups", "ctx", None),
        P("groups", None, "ctx"),
        P("groups"),
    )
    return jax.shard_map(
        functools.partial(local, mesh.shape["ctx"]), mesh=mesh, in_specs=placed,
        out_specs=P("groups", None), check_vma=False,
    )
```
